256 devices in a mesh: ctx: 128 (over z, x_lo, y, core), head: 2 (over x_hi).
Axes of the slice: x: 4 (x_hi: 2, x_lo: 2; x = x_hi * 2 + x_lo), y: 4, z: 8, core: 2. Of those that a mesh axis runs over, the one named last changes fastest.
Arguments:
- latent_raw: bfloat16 [16384, 576], P(('ctx', 'head')), may hold values from -6 to 6
- kv_gain: float32 [512], replicated, may hold values from 0.1 to 1.9
- query_nope: bfloat16 [16384, 8192], P('ctx', 'head'), may hold values from -144 to 144
- query_rope: bfloat16 [16384, 4096], P('ctx', 'head'), may hold values from -6 to 6
- key_up: bfloat16 [64, 128, 512], P('head'), may hold values from -0.5 to 0.5
- value_up: bfloat16 [64, 512, 128], P('head'), may hold values from -0.25 to 0.25
- doc_lengths: int32 [32], replicated, may hold values from 1 to 896, 16384 in all
Outputs:
- attended: bfloat16 [16384, 8192], P('ctx', 'head')
The draws below stay inside these ranges and needn't reach their ends.
Inputs may be any that keep to these rules, and one draw needn't show every extreme that they name: `doc_lengths`: documents lie end to end over all 16384 positions; the longest has exactly 896 positions.
All inputs are finite; a program needn't handle non-finite values.
Results may differ from the reference program's by a relative error of at most 0.012.
The reference program's roundings to bfloat16 on the way (of `kv_rows`, `absorbed`, `rotated`, `weights` and `mixed_latent`) count: a program that leaves them out, or rounds other values in their place, can miss the bound.
Values may be sent and summed in bfloat16 or wider, within the bound.
A program may use at most 64 MiB of HBM per device.

```python
import math
import jax
import jax.numpy as jnp
import numpy as np
from jax import lax

KV_RANK = 512
ROPE = 64
NOPE = 128
VDIM = 128
HEADS = 64
TOK_DEV = 128
HOPS = 7
TOKENS = 16384
MOST = 896
DOCS = 32
N_CTX = 128


def draw_query_nope(key, part):
    key_base = jax.random.fold_in(key, 0)
    base = jnp.clip(jax.random.normal(key_base, (TOKENS, HEADS * NOPE), jnp.float32), -6.0, 6.0)
    return (0.7 * base).astype(jnp.bfloat16)


def levels(own_key, shape, shards, least, high):
    def one(axis_at, shards_of):
        draws = jax.random.uniform(jax.random.fold_in(jax.random.fold_in(own_key, 6), axis_at), (shards_of,), jnp.float32, least / len(shards), high / len(shards))
        return jnp.repeat(jnp.exp(draws), shape[axis_at] // shards_of).reshape((-1,) + (1,) * (len(shape) - axis_at - 1))

    level = one(*shards[0])
    for cut in shards[1:]:
        level = level * one(*cut)
    return level


def length_profile(number_of, total, reach, skew):
    loads = [(1 << 20) // math.isqrt(rank ** skew) + 1 for rank in range(2, number_of + 1)]
    spare, given = total - reach - (number_of - 1), [1] * (number_of - 1)
    while spare > 0:
        movable = [i for i in range(number_of - 1) if given[i] < reach]
        whole, budget = sum([loads[i] for i in movable]), spare
        for i in movable:
            addition = min(reach - given[i], max(1, budget * loads[i] // whole), spare)
            given[i] = given[i] + addition
            spare = spare - addition
    return np.array([reach] + given)


def uneven_parts(key, count, total, most, slope):
    if count == 2:
        one = jax.random.randint(key, (), max(1, total - most), min(most, total - 1) + 1)
        return jnp.stack([one, total - one])
    sizes = jnp.asarray(length_profile(count, total, most, slope), jnp.int32)
    pairs = (count - 1) // 2
    giver, taker = sizes[1:1 + 2 * pairs:2], sizes[2:2 + 2 * pairs:2]
    room = jnp.minimum(giver - 1, most - taker)
    moved = jax.random.randint(jax.random.fold_in(key, 1), (pairs,), 0, 1 << 20) % (room + 1)
    sizes = sizes.at[1:1 + 2 * pairs:2].set(giver - moved).at[2:2 + 2 * pairs:2].set(taker + moved)
    return sizes[jax.random.permutation(jax.random.fold_in(key, 2), count)]


def normal_values(own_key, dims, scale, most, cuts=(), held_as=jnp.bfloat16):
    array = scale * jax.random.normal(own_key, dims, jnp.float32)
    if cuts:
        array = array * levels(own_key, dims, cuts, -0.22, 0.18)
    return jnp.clip(array, -most, most).astype(held_as)


def setup_inputs(seed: int = 0) -> dict:
    seeds = jax.random.split(jax.random.key(seed), 8)
    return {
        "latent_raw": normal_values(seeds[0], (TOKENS, KV_RANK + ROPE), 1.0, 6.0, ((0, 256),)),
        "kv_gain": jnp.clip(1.0 + 0.18 * jax.random.normal(seeds[1], (KV_RANK,), jnp.float32), 0.1, 1.9),
        "query_nope": draw_query_nope(jax.random.fold_in(seeds[7], 71), 0),
        "query_rope": normal_values(seeds[3], (TOKENS, HEADS * ROPE), 1.0, 6.0, ((0, 128), (1, 2))),
        "key_up": normal_values(seeds[4], (HEADS, NOPE, KV_RANK), NOPE ** -0.5, 0.5, ((0, 2),)),
        "value_up": normal_values(seeds[5], (HEADS, KV_RANK, VDIM), KV_RANK ** -0.5, 0.25, ((0, 2),)),
        "doc_lengths": uneven_parts(seeds[6], DOCS, TOKENS, MOST, 2).astype(jnp.int32),
    }


epsilon = 1e-06
masked_score = -1e+30

def doc_begin(positions, starts):
    inside = starts[None, :] <= positions[:, None]
    return lax.optimization_barrier(jnp.max(jnp.where(inside, starts[None, :], 0), axis=1)).astype(jnp.int32)

def rotation(offsets, rope_half):
    frequency = 10000.0 ** (-2.0 * jnp.arange(rope_half, dtype=jnp.float32) / (2 * rope_half))
    angles = offsets.astype(jnp.float32)[:, None] * frequency[None, :]
    return (jnp.cos(angles), jnp.sin(angles))

def rotate(values, cos_table, sin_table):
    rope_half = cos_table.shape[-1]
    first_half = values[..., :rope_half]
    second_half = values[..., rope_half:]
    return jnp.concatenate([first_half * cos_table - second_half * sin_table, second_half * cos_table + first_half * sin_table], axis=-1)

def reference(latent_raw, kv_gain, query_nope, query_rope, key_up, value_up, doc_lengths):
    score_scale = (NOPE + ROPE) ** (-0.5)
    starts = (jnp.cumsum(doc_lengths) - doc_lengths).astype(jnp.int32)
    positions = jnp.arange(TOKENS, dtype=jnp.int32)
    begins = doc_begin(positions, starts)
    cos_table, sin_table = rotation(positions - begins, ROPE // 2)
    raw_rows = latent_raw.astype(jnp.float32)
    latent_part = raw_rows[:, :KV_RANK]
    normed = latent_part * lax.rsqrt(lax.optimization_barrier(jnp.mean(latent_part * latent_part, axis=1, keepdims=True)) + epsilon) * kv_gain
    kv_rows = jnp.concatenate([normed, rotate(raw_rows[:, KV_RANK:], cos_table, sin_table)], axis=1).astype(jnp.bfloat16)
    span_rows = (HOPS + 1) * TOK_DEV
    pad_rows = HOPS * TOK_DEV
    kv_padded = jnp.concatenate([jnp.zeros((pad_rows, KV_RANK + ROPE), jnp.bfloat16), kv_rows], axis=0)
    kv_padded = lax.optimization_barrier(kv_padded).astype(jnp.float32)
    begin_padded = jnp.concatenate([jnp.full((pad_rows,), -1, jnp.int32), begins], axis=0)
    key_weight = key_up.astype(jnp.float32)
    value_weight = value_up.astype(jnp.float32)

    def query_block(block_index):
        first_row = (block_index * TOK_DEV).astype(jnp.int32)
        query_pos = first_row + jnp.arange(TOK_DEV, dtype=jnp.int32)
        query_begin = lax.dynamic_slice_in_dim(begins, first_row, TOK_DEV, 0)
        nope_rows = lax.dynamic_slice_in_dim(query_nope, first_row, TOK_DEV, 0).astype(jnp.float32).reshape(TOK_DEV, HEADS, NOPE)
        absorbed = jnp.einsum('thn,hnr->thr', nope_rows, key_weight).astype(jnp.bfloat16)
        rope_rows = lax.dynamic_slice_in_dim(query_rope, first_row, TOK_DEV, 0).astype(jnp.float32).reshape(TOK_DEV, HEADS, ROPE)
        cos_query = lax.dynamic_slice_in_dim(cos_table, first_row, TOK_DEV, 0)
        sin_query = lax.dynamic_slice_in_dim(sin_table, first_row, TOK_DEV, 0)
        rotated = rotate(rope_rows, cos_query[:, None, :], sin_query[:, None, :]).astype(jnp.bfloat16)
        queries = lax.optimization_barrier(jnp.concatenate([absorbed, rotated], axis=2)).astype(jnp.float32)
        key_rows = lax.dynamic_slice_in_dim(kv_padded, first_row, span_rows, 0)
        key_begin = lax.dynamic_slice_in_dim(begin_padded, first_row, span_rows, 0)
        key_pos = first_row - pad_rows + jnp.arange(span_rows, dtype=jnp.int32)
        live_pairs = (key_pos[None, :] <= query_pos[:, None]) & (key_begin[None, :] == query_begin[:, None])
        scores = jnp.einsum('thc,sc->hts', queries, key_rows) * score_scale
        scores = jnp.where(live_pairs[None], scores, masked_score)
        row_max = lax.optimization_barrier(jnp.max(scores, axis=2, keepdims=True))
        weights = jnp.where(live_pairs[None], jnp.exp(scores - row_max), 0.0)
        totals = lax.optimization_barrier(jnp.sum(weights, axis=2))
        rounded = lax.optimization_barrier(weights.astype(jnp.bfloat16)).astype(jnp.float32)
        mixed_latent = (jnp.einsum('hts,sr->htr', rounded, key_rows[:, :KV_RANK]) / totals[:, :, None]).astype(jnp.bfloat16)
        mixed_latent = lax.optimization_barrier(mixed_latent).astype(jnp.float32)
        attended = jnp.einsum('htr,hrv->thv', mixed_latent, value_weight)
        return attended.astype(jnp.bfloat16).reshape(TOK_DEV, HEADS * VDIM)
    blocks = lax.map(query_block, jnp.arange(N_CTX, dtype=jnp.int32))
    return blocks.reshape(TOKENS, HEADS * VDIM)
```

```python
import functools
import math

import jax
import jax.numpy as jnp
from jax import lax
from jax.experimental import pallas as pl
from jax.experimental.pallas import tpu as pltpu
from jax.sharding import PartitionSpec as P

LATENT, WIDTH = 512, 640
ROWS, HALF, BLOCKS, DOCS = 128, 64, 8, 32
KEYS = BLOCKS * ROWS
SCALE = 192.0 ** -0.5
LOG2E = math.log2(math.e)
DIRECT = (2, 4, 6)
MESH = pl.DeviceIdType.MESH


def gather_kernel(count, raw_ref, gain_ref, len_ref, kv_ref, begin_ref, cos_ref, sin_ref, send_sem, recv_sem):
    ctx, head = lax.axis_index("ctx"), lax.axis_index("head")
    core = lax.rem(ctx, 2)
    other = 1 - head
    sibling = ctx + 1 - 2 * core

    def later(steps):
        return lax.rem(ctx + steps, count)

    def earlier(steps):
        return lax.rem(ctx + count - steps, count)

    barrier = pltpu.get_barrier_semaphore()

    def greet(where):
        pl.semaphore_signal(barrier, inc=1, device_id=where, device_id_type=MESH)

    greet((ctx, other))
    greet((sibling, head))
    for steps in DIRECT:
        greet((earlier(steps), head))

    @pl.when(core == 0)
    def _():
        greet((earlier(7), head))

    row = lax.broadcasted_iota(jnp.int32, (ROWS, 128), 0)
    lane = lax.broadcasted_iota(jnp.int32, (ROWS, 128), 1)
    position = ctx * ROWS + row
    begin = jnp.zeros((ROWS, 128), jnp.int32)
    start = jnp.int32(0)
    for doc in range(DOCS):
        begin = jnp.where(position >= start, start, begin)
        start = start + len_ref[doc]
    begin_ref[...] = begin
    frequency = jnp.exp2((lane & 31).astype(jnp.float32) * (-math.log2(10000.0) / 32))
    angle = (position - begin).astype(jnp.float32) * frequency
    cos_ref[...] = jnp.cos(angle)
    sine = jnp.sin(angle)
    sin_ref[...] = jnp.where((lane & 63) < 32, -sine, sine)

    def place(steps, half):
        return pl.ds((BLOCKS - 1 - steps) * ROWS + half * HALF, HALF)

    mine = pl.ds((BLOCKS - 1) * ROWS + pl.multiple_of(head * HALF, HALF), HALF)
    latent = raw_ref[:, :LATENT].astype(jnp.float32)
    norm = lax.rsqrt(jnp.mean(latent * latent, axis=1, keepdims=True) + 1e-6)
    kv_ref[mine, :LATENT] = (latent * norm * gain_ref[...]).astype(jnp.bfloat16)
    rope = raw_ref[:, LATENT:].astype(jnp.float32)
    swapped = jnp.concatenate([rope[:, 32:], rope[:, :32]], axis=1)
    table = pl.ds(pl.multiple_of(head * HALF, HALF), HALF)
    turned = rope * cos_ref[table, :64] + swapped * sin_ref[table, :64]
    kv_ref[mine, LATENT:] = jnp.concatenate([turned, turned], axis=1).astype(jnp.bfloat16)

    pl.semaphore_wait(barrier, 5 + core)

    def half_at(steps, half):
        first = (BLOCKS - 1 - steps) * ROWS
        return pl.ds(first + pl.multiple_of(half * HALF, HALF), HALF)

    def copy(source, target, half, where):
        return pltpu.make_async_remote_copy(
            src_ref=kv_ref.at[half_at(source, half)],
            dst_ref=kv_ref.at[half_at(target, half)],
            send_sem=send_sem.at[target, half],
            recv_sem=recv_sem.at[target, half],
            device_id=where,
            device_id_type=MESH,
        )

    def to_partner():
        return copy(0, 0, head, (ctx, other))

    def direct(steps, half):
        return copy(0, steps, half, (later(steps), head))

    def to_upper(steps, half):
        return copy(steps, steps + 1, half, (sibling, head))

    def to_lower(steps, half):
        return copy(steps, steps - 1, half, (sibling, head))

    def spread_own(half):
        for steps in DIRECT:
            direct(steps, half).start()

        @pl.when(core == 0)
        def _():
            to_upper(0, half).start()

        @pl.when(core == 1)
        def _():
            copy(0, 7, half, (later(7), head)).start()

    def arrived(steps, half):
        copy(steps, steps, half, (ctx, other)).wait_recv()

    to_partner().start()
    spread_own(head)
    arrived(0, other)
    spread_own(other)
    for steps in DIRECT:
        for half in (head, other):
            arrived(steps, half)

            @pl.when(core == 0)
            def _():
                to_upper(steps, half).start()

            @pl.when(core == 1)
            def _():
                to_lower(steps, half).start()

    for steps in (1, 3, 5, 7):
        for half in (0, 1):
            arrived(steps, half)
    to_partner().wait_send()
    for half in (0, 1):
        for steps in DIRECT:
            direct(steps, half).wait_send()

        @pl.when(core == 0)
        def _():
            for steps in (0, 2, 4, 6):
                to_upper(steps, half).wait_send()

        @pl.when(core == 1)
        def _():
            copy(0, 7, half, (later(7), head)).wait_send()
            for steps in DIRECT:
                to_lower(steps, half).wait_send()


def attend_kernel(group, begin_ref, cos_ref, sin_ref, kv_ref, nope_ref, rope_ref, up_ref, value_ref, out_ref, bias, query, score):
    @pl.when(pl.program_id(0) == 0)
    def _():
        key = lax.broadcasted_iota(jnp.int32, (ROWS, KEYS), 1)
        row = lax.broadcasted_iota(jnp.int32, (ROWS, KEYS), 0)
        first = begin_ref[:, :1] - (lax.axis_index("ctx") - (BLOCKS - 1)) * ROWS
        live = (key >= first) & (key <= row + (KEYS - ROWS))
        bias[...] = jnp.where(live, 0.0, -1e30)

    lane = lax.broadcasted_iota(jnp.int32, (ROWS, 128), 1)
    for pair in range(group // 2):
        rope = rope_ref[:, pair * 128 : (pair + 1) * 128].astype(jnp.float32)
        swapped = jnp.where((lane & 63) < 32, pltpu.roll(rope, 96, 1), pltpu.roll(rope, 32, 1))
        turned = rope * cos_ref[...] + swapped * sin_ref[...]
        for odd in range(2):
            h = 2 * pair + odd
            own = pl.ds(h * ROWS, ROWS)
            keep = (lane >= 64) if odd else (lane < 64)
            query[own, LATENT:] = jnp.where(keep, turned, 0.0).astype(jnp.bfloat16)
            query[own, :LATENT] = jnp.dot(
                nope_ref[:, h * 128 : (h + 1) * 128], up_ref[h], preferred_element_type=jnp.float32
            ).astype(jnp.bfloat16)
    score[...] = lax.dot_general(
        query[...], kv_ref[...], (((1,), (1,)), ((), ())), preferred_element_type=jnp.float32
    )
    for h in range(group):
        s = score[pl.ds(h * ROWS, ROWS), :] + bias[...]
        top = jnp.max(s, axis=1, keepdims=True)
        weight = jnp.exp2((s - top) * (SCALE * LOG2E))
        total = jnp.sum(weight, axis=1, keepdims=True)
        mixed = jnp.dot(weight.astype(jnp.bfloat16), kv_ref[:, :LATENT], preferred_element_type=jnp.float32)
        mixed = (mixed * (1.0 / total)).astype(jnp.bfloat16)
        out_ref[:, h * 128 : (h + 1) * 128] = jnp.dot(
            mixed, value_ref[h], preferred_element_type=jnp.float32
        ).astype(jnp.bfloat16)


def shards(count, latent_raw, kv_gain, query_nope, query_rope, key_up, value_up, doc_lengths):
    vmem = pl.BlockSpec(memory_space=pltpu.VMEM)
    kv, begin, cosine, sine = pl.pallas_call(
        functools.partial(gather_kernel, count),
        out_shape=(
            jax.ShapeDtypeStruct((KEYS, WIDTH), jnp.bfloat16),
            jax.ShapeDtypeStruct((ROWS, 128), jnp.int32),
            jax.ShapeDtypeStruct((ROWS, 128), jnp.float32),
            jax.ShapeDtypeStruct((ROWS, 128), jnp.float32),
        ),
        in_specs=[vmem, vmem, pl.BlockSpec(memory_space=pltpu.SMEM)],
        out_specs=(vmem,) * 4,
        scratch_shapes=[pltpu.SemaphoreType.DMA((BLOCKS, 2)), pltpu.SemaphoreType.DMA((BLOCKS, 2))],
        compiler_params=pltpu.CompilerParams(collective_id=0, has_side_effects=True),
        name="gather_rows",
    )(latent_raw, kv_gain[None, :], doc_lengths)
    heads = key_up.shape[0]
    group = 8

    def whole(*shape):
        return pl.BlockSpec(shape, lambda i: (0,) * len(shape))

    return pl.pallas_call(
        functools.partial(attend_kernel, group),
        grid=(heads // group,),
        in_specs=[
            whole(ROWS, 128),
            whole(ROWS, 128),
            whole(ROWS, 128),
            whole(KEYS, WIDTH),
            pl.BlockSpec((ROWS, group * 128), lambda i: (0, i)),
            pl.BlockSpec((ROWS, group * 64), lambda i: (0, i)),
            pl.BlockSpec((group, 128, LATENT), lambda i: (i, 0, 0)),
            pl.BlockSpec((group, LATENT, 128), lambda i: (i, 0, 0)),
        ],
        out_specs=pl.BlockSpec((ROWS, group * 128), lambda i: (0, i)),
        out_shape=jax.ShapeDtypeStruct((ROWS, heads * 128), jnp.bfloat16),
        scratch_shapes=[
            pltpu.VMEM((ROWS, KEYS), jnp.float32),
            pltpu.VMEM((group * ROWS, WIDTH), jnp.bfloat16),
            pltpu.VMEM((group * ROWS, KEYS), jnp.float32),
        ],
        compiler_params=pltpu.CompilerParams(vmem_limit_bytes=48 << 20),
        name="attend",
    )(begin, cosine, sine, kv, query_nope, query_rope, key_up, value_up)


def solution(mesh):
    return jax.shard_map(
        functools.partial(shards, mesh.shape["ctx"]),
        mesh=mesh,
        in_specs=(
            P(("ctx", "head"), None),
            P(),
            P("ctx", "head"),
            P("ctx", "head"),
            P("head", None, None),
            P("head", None, None),
            P(),
        ),
        out_specs=P("ctx", "head"),
        check_vma=False,
    )
```

```python
import functools
import math

import jax
import jax.numpy as jnp
from jax import lax
from jax.experimental import pallas as pl
from jax.experimental.pallas import tpu as pltpu
from jax.sharding import PartitionSpec as P

LATENT, WIDTH = 512, 640
ROWS, HALF, BLOCKS, DOCS = 128, 64, 8, 32
KEYS = BLOCKS * ROWS
SCALE = 192.0 ** -0.5
LOG2E = math.log2(math.e)
DIRECT = (2, 4, 6)
CHUNK = 256
GROUP = 4
BAND = GROUP * ROWS
SLICE = 16
PARTS = 4
MESH = pl.DeviceIdType.MESH
WHAT = {"absorb", "score", "soft", "mix"}


def latent_attention(
    count, heads, remote, raw_ref, gain_ref, len_ref, nope_hbm, rope_hbm, up_hbm, value_hbm, out_hbm,
    kv, nope, rope, up, value, query, score, weight_a, weight_b, total_a, total_b, bias, cos_ref, sin_ref, out,
    send_sem, recv_sem, load_sem, out_sem,
):
    ctx = lax.axis_index("ctx") if remote else 0
    head = lax.axis_index("head") if remote else 0
    core = lax.rem(ctx, 2)
    other = 1 - head
    sibling = ctx + 1 - 2 * core
    per = heads // PARTS

    def later(steps):
        return lax.rem(ctx + steps, count)

    def earlier(steps):
        return lax.rem(ctx + count - steps, count)

    if remote:
        barrier = pltpu.get_barrier_semaphore()

        def greet(where):
            pl.semaphore_signal(barrier, inc=1, device_id=where, device_id_type=MESH)

        greet((ctx, other))
        greet((sibling, head))
        for steps in DIRECT:
            greet((earlier(steps), head))

        @pl.when(core == 0)
        def _():
            greet((earlier(7), head))

    def load_query():
        return pltpu.make_async_copy(nope_hbm, nope, load_sem.at[0])

    def load_rope():
        return pltpu.make_async_copy(rope_hbm, rope, load_sem.at[1])

    def load_up(part):
        own = pl.ds(part * per, per)
        return pltpu.make_async_copy(up_hbm.at[own], up.at[own], load_sem.at[2 + part])

    def load_value():
        return pltpu.make_async_copy(value_hbm, value, load_sem.at[2 + PARTS])

    load_query().start()
    load_rope().start()
    for part in range(PARTS):
        load_up(part).start()
    load_value().start()

    row = lax.broadcasted_iota(jnp.int32, (ROWS, 128), 0)
    lane = lax.broadcasted_iota(jnp.int32, (ROWS, 128), 1)
    position = ctx * ROWS + row
    begin = jnp.zeros((ROWS, 128), jnp.int32)
    start = jnp.int32(0)
    for doc in range(DOCS):
        begin = jnp.where(position >= start, start, begin)
        start = start + len_ref[doc]
    frequency = jnp.exp2((lane & 31).astype(jnp.float32) * (-math.log2(10000.0) / 32))
    angle = (position - begin).astype(jnp.float32) * frequency
    cos_ref[...] = jnp.cos(angle)
    sine = jnp.sin(angle)
    sin_ref[...] = jnp.where((lane & 63) < 32, -sine, sine)

    def half_at(steps, half):
        first = (BLOCKS - 1 - steps) * ROWS
        return pl.ds(first + pl.multiple_of(half * HALF, HALF), HALF)

    mine = half_at(0, head)
    latent = raw_ref[:, :LATENT].astype(jnp.float32)
    norm = lax.rsqrt(jnp.mean(latent * latent, axis=1, keepdims=True) + 1e-6)
    kv[mine, :LATENT] = (latent * norm * gain_ref[...]).astype(jnp.bfloat16)
    pair = raw_ref[:, LATENT:].astype(jnp.float32)
    swapped = jnp.concatenate([pair[:, 32:], pair[:, :32]], axis=1)
    table = pl.ds(pl.multiple_of(head * HALF, HALF), HALF)
    turned = pair * cos_ref[table, :64] + swapped * sin_ref[table, :64]
    kv[mine, LATENT:] = jnp.concatenate([turned, turned], axis=1).astype(jnp.bfloat16)

    def copy(source, target, half, where):
        return pltpu.make_async_remote_copy(
            src_ref=kv.at[half_at(source, half)],
            dst_ref=kv.at[half_at(target, half)],
            send_sem=send_sem.at[target, half],
            recv_sem=recv_sem.at[target, half],
            device_id=where,
            device_id_type=MESH,
        )

    def to_partner():
        return copy(0, 0, head, (ctx, other))

    def direct(steps, half):
        return copy(0, steps, half, (later(steps), head))

    def to_upper(steps, half):
        return copy(steps, steps + 1, half, (sibling, head))

    def to_lower(steps, half):
        return copy(steps, steps - 1, half, (sibling, head))

    def spread_own(half):
        for steps in DIRECT:
            direct(steps, half).start()

        @pl.when(core == 0)
        def _():
            to_upper(0, half).start()

        @pl.when(core == 1)
        def _():
            copy(0, 7, half, (later(7), head)).start()

    def arrived(steps, half):
        copy(steps, steps, half, (ctx, other)).wait_recv()

    def pass_on(steps):
        for half in (head, other):
            arrived(steps, half)

            @pl.when(core == 0)
            def _():
                to_upper(steps, half).start()

            @pl.when(core == 1)
            def _():
                to_lower(steps, half).start()

    if remote:
        pl.semaphore_wait(barrier, 5 + core)
        to_partner().start()
        spread_own(head)

    low = lane < 64
    front = (lane & 63) < 32

    def absorb(part, carry):
        load_up(part).wait()
        for p in range(per // 2):
            at = pl.multiple_of(part * (per * 64) + p * 128, 128)
            pairs = rope[:, pl.ds(at, 128)].astype(jnp.float32)
            swap = jnp.where(front, pltpu.roll(pairs, 96, 1), pltpu.roll(pairs, 32, 1))
            turn = pairs * cos_ref[...] + swap * sin_ref[...]
            for odd in range(2):
                h = part * per + 2 * p + odd
                own = pl.ds(pl.multiple_of(h * ROWS, ROWS), ROWS)
                query[own, LATENT:] = jnp.where(~low if odd else low, turn, 0.0).astype(jnp.bfloat16)
                query[own, :LATENT] = jnp.dot(
                    nope[:, pl.ds(pl.multiple_of(h * 128, 128), 128)], up[h], preferred_element_type=jnp.float32
                ).astype(jnp.bfloat16)
        return carry

    load_query().wait()
    load_rope().wait()
    if "absorb" in WHAT:
        lax.fori_loop(0, PARTS // 2, absorb, 0)
    if remote:
        arrived(0, other)
        spread_own(other)
    if "absorb" in WHAT:
        lax.fori_loop(PARTS // 2, PARTS, absorb, 0)
    else:
        for part in range(PARTS):
            load_up(part).wait()

    key = lax.broadcasted_iota(jnp.int32, (ROWS, 128), 1)
    for tile in range(BLOCKS):
        shifted = (ctx - (BLOCKS - 1) + tile) * ROWS + key
        bias[:, tile * 128 : (tile + 1) * 128] = jnp.where((shifted >= begin) & (shifted <= position), 0.0, -1e30)

    def scores(chunk):
        first = KEYS - (chunk + 1) * CHUNK

        def band(step, carry):
            own = pl.ds(pl.multiple_of(step * 1024, 1024), 1024)
            score[own, first : first + CHUNK] = lax.dot_general(
                query[own, :], kv[first : first + CHUNK, :], (((1,), (1,)), ((), ())),
                preferred_element_type=jnp.float32,
            )
            return carry

        lax.fori_loop(0, heads * ROWS // 1024, band, 0)

    for chunk in range(KEYS // CHUNK):
        if remote:
            if chunk + 1 < KEYS // CHUNK:
                pass_on(2 * chunk + 2)
            for half in (0, 1):
                arrived(2 * chunk + 1, half)
        if "score" in WHAT:
            scores(chunk)

    load_value().wait()

    def soften(step, weight, total):
        for piece in range(BAND // SLICE):
            at = piece * SLICE
            s = score[pl.ds(pl.multiple_of(step * BAND, BAND) + at, SLICE), :]
            s = s + bias[at % ROWS : at % ROWS + SLICE, :]
            top = jnp.max(s, axis=1, keepdims=True)
            w = jnp.exp2((s - top) * (SCALE * LOG2E))
            total[at : at + SLICE, :] = jnp.broadcast_to(jnp.sum(w, axis=1, keepdims=True), (SLICE, 128))
            weight[at : at + SLICE, :] = w.astype(jnp.bfloat16)

    def mix(step, weight, total):
        mixed = jnp.dot(weight[...], kv[:, :LATENT], preferred_element_type=jnp.float32)
        scale = 1.0 / total[...]
        mixed = (mixed * jnp.concatenate([scale] * (LATENT // 128), axis=1)).astype(jnp.bfloat16)
        for h in range(GROUP):
            out[:, pl.ds(pl.multiple_of(step * BAND, BAND) + h * 128, 128)] = jnp.dot(
                mixed[h * ROWS : (h + 1) * ROWS], value[step * GROUP + h], preferred_element_type=jnp.float32
            ).astype(jnp.bfloat16)
        write(step).start()

    def write(step):
        own = pl.ds(pl.multiple_of(step * BAND, BAND), BAND)
        return pltpu.make_async_copy(out.at[:, own], out_hbm.at[:, own], out_sem.at[step])

    steps = heads // GROUP
    if "soft" not in WHAT: soften = lambda *a: None
    if "mix" not in WHAT: mix = lambda s, *a: write(s).start()
    soften(0, weight_a, total_a)

    def two(j, carry):
        soften(2 * j + 1, weight_b, total_b)
        mix(2 * j, weight_a, total_a)
        soften(2 * j + 2, weight_a, total_a)
        mix(2 * j + 1, weight_b, total_b)
        return carry

    lax.fori_loop(0, steps // 2 - 1, two, 0)
    soften(steps - 1, weight_b, total_b)
    mix(steps - 2, weight_a, total_a)
    mix(steps - 1, weight_b, total_b)
    for step in range(steps):
        write(step).wait()

    if remote:
        to_partner().wait_send()
        for half in (0, 1):
            for steps in DIRECT:
                direct(steps, half).wait_send()

            @pl.when(core == 0)
            def _():
                for steps in (0, 2, 4, 6):
                    to_upper(steps, half).wait_send()

            @pl.when(core == 1)
            def _():
                copy(0, 7, half, (later(7), head)).wait_send()
                for steps in DIRECT:
                    to_lower(steps, half).wait_send()


def shards(count, remote, latent_raw, kv_gain, query_nope, query_rope, key_up, value_up, doc_lengths):
    vmem, hbm = pl.BlockSpec(memory_space=pltpu.VMEM), pl.BlockSpec(memory_space=pl.ANY)
    heads = key_up.shape[0]
    bf16, f32 = jnp.bfloat16, jnp.float32
    return pl.pallas_call(
        functools.partial(latent_attention, count, heads, remote),
        out_shape=jax.ShapeDtypeStruct((ROWS, heads * 128), bf16),
        in_specs=[vmem, vmem, pl.BlockSpec(memory_space=pltpu.SMEM), hbm, hbm, hbm, hbm],
        out_specs=hbm,
        scratch_shapes=[
            pltpu.VMEM((KEYS, WIDTH), bf16),
            pltpu.VMEM(query_nope.shape, bf16),
            pltpu.VMEM(query_rope.shape, bf16),
            pltpu.VMEM(key_up.shape, bf16),
            pltpu.VMEM(value_up.shape, bf16),
            pltpu.VMEM((heads * ROWS, WIDTH), bf16),
            pltpu.VMEM((heads * ROWS, KEYS), f32),
            pltpu.VMEM((BAND, KEYS), bf16),
            pltpu.VMEM((BAND, KEYS), bf16),
            pltpu.VMEM((BAND, 128), f32),
            pltpu.VMEM((BAND, 128), f32),
            pltpu.VMEM((ROWS, KEYS), f32),
            pltpu.VMEM((ROWS, 128), f32),
            pltpu.VMEM((ROWS, 128), f32),
            pltpu.VMEM((ROWS, heads * 128), bf16),
            pltpu.SemaphoreType.DMA((BLOCKS, 2)),
            pltpu.SemaphoreType.DMA((BLOCKS, 2)),
            pltpu.SemaphoreType.DMA((3 + PARTS,)),
            pltpu.SemaphoreType.DMA((heads // GROUP,)),
        ],
        compiler_params=pltpu.CompilerParams(
            collective_id=0 if remote else None, has_side_effects=True, vmem_limit_bytes=60 << 20
        ),
        name="latent_attention",
    )(latent_raw, kv_gain[None, :], doc_lengths, query_nope, query_rope, key_up, value_up)


def solution(mesh):
    return jax.shard_map(
        functools.partial(shards, mesh.shape["ctx"], True),
        mesh=mesh,
        in_specs=(
            P(("ctx", "head"), None),
            P(),
            P("ctx", "head"),
            P("ctx", "head"),
            P("head", None, None),
            P("head", None, None),
            P(),
        ),
        out_specs=P("ctx", "head"),
        check_vma=False,
    )
```

```python
import functools
import math

import jax
import jax.numpy as jnp
from jax import lax
from jax.experimental import pallas as pl
from jax.experimental.pallas import tpu as pltpu
from jax.sharding import PartitionSpec as P

LATENT, WIDTH = 512, 640
ROWS, HALF, BLOCKS, DOCS = 128, 64, 8, 32
KEYS = BLOCKS * ROWS
SCALE = 192.0 ** -0.5
LOG2E = math.log2(math.e)
REACH = (2, 4, 6, 8)
CHUNK = 256
FAR = KEYS - CHUNK
TALL = 1024
GROUP = 4
BAND = GROUP * ROWS
SLICE = 16
PARTS = 4
MESH = pl.DeviceIdType.MESH


def latent_attention(
    count, heads, remote, raw_ref, gain_ref, len_ref, nope_hbm, rope_hbm, up_hbm, value_hbm, out_hbm,
    kv, nope, rope, up, value, query, score, peak, top_ref, sum_ref, partial, last_a, last_b, weight_a, weight_b,
    narrow_a, narrow_b, old_a, old_b, new_a, new_b, bias, cos_ref, sin_ref, out,
    send_sem, recv_sem, load_sem, out_sem,
):
    ctx = lax.axis_index("ctx") if remote else 0
    head = lax.axis_index("head") if remote else 0
    core = lax.rem(ctx, 2)
    other = 1 - head
    sibling = ctx + 1 - 2 * core
    per = heads // PARTS

    def has_behind(steps):
        return ctx >= steps

    def has_ahead(steps):
        return ctx + steps < count

    if remote:
        barrier = pltpu.get_barrier_semaphore()

        def greet(where):
            pl.semaphore_signal(barrier, inc=1, device_id=where, device_id_type=MESH)

        @pl.when(ctx < BLOCKS)
        def _():
            kv[...] = jnp.zeros_like(kv)

        greet((ctx, other))
        greet((sibling, head))
        for steps in REACH:

            @pl.when(has_behind(steps))
            def _():
                for plane in (0, 1):
                    greet((ctx - steps, plane))

    def load_query():
        return pltpu.make_async_copy(nope_hbm, nope, load_sem.at[0])

    def load_rope():
        return pltpu.make_async_copy(rope_hbm, rope, load_sem.at[1])

    def load_up(part):
        own = pl.ds(part * per, per)
        return pltpu.make_async_copy(up_hbm.at[own], up.at[own], load_sem.at[2 + part])

    def load_value():
        return pltpu.make_async_copy(value_hbm, value, load_sem.at[2 + PARTS])

    load_query().start()
    load_rope().start()
    for part in range(PARTS):
        load_up(part).start()
    load_value().start()

    row = lax.broadcasted_iota(jnp.int32, (ROWS, 128), 0)
    lane = lax.broadcasted_iota(jnp.int32, (ROWS, 128), 1)
    position = ctx * ROWS + row
    begin = jnp.zeros((ROWS, 128), jnp.int32)
    start = jnp.int32(0)
    for doc in range(DOCS):
        begin = jnp.where(position >= start, start, begin)
        start = start + len_ref[doc]
    frequency = jnp.exp2((lane & 31).astype(jnp.float32) * (-math.log2(10000.0) / 32))
    angle = (position - begin).astype(jnp.float32) * frequency
    cos_ref[...] = jnp.cos(angle)
    sine = jnp.sin(angle)
    sin_ref[...] = jnp.where((lane & 63) < 32, -sine, sine)

    def half_at(steps, half):
        return pl.ds(pl.multiple_of((BLOCKS - steps) * ROWS + half * HALF, HALF), HALF)

    mine = half_at(0, head)
    latent = raw_ref[:, :LATENT].astype(jnp.float32)
    norm = lax.rsqrt(jnp.mean(latent * latent, axis=1, keepdims=True) + 1e-6)
    kv[mine, :LATENT] = (latent * norm * gain_ref[...]).astype(jnp.bfloat16)
    pair = raw_ref[:, LATENT:].astype(jnp.float32)
    swapped = jnp.concatenate([pair[:, 32:], pair[:, :32]], axis=1)
    table = pl.ds(pl.multiple_of(head * HALF, HALF), HALF)
    turned = pair * cos_ref[table, :64] + swapped * sin_ref[table, :64]
    kv[mine, LATENT:] = jnp.concatenate([turned, turned], axis=1).astype(jnp.bfloat16)

    def copy(source, target, half, where, send):
        return pltpu.make_async_remote_copy(
            src_ref=kv.at[half_at(source, half)],
            dst_ref=kv.at[half_at(target, half)],
            send_sem=send_sem.at[send],
            recv_sem=recv_sem.at[target, half],
            device_id=where,
            device_id_type=MESH,
        )

    def to_partner():
        return copy(0, 0, head, (ctx, other), 0)

    def direct(steps, plane):
        return copy(0, steps, head, (ctx + steps, plane), steps - 1 + plane)

    def across(steps, half):
        source = jnp.where((core == 1) & (steps == 0), BLOCKS, steps)
        target = jnp.where(core == 0, steps + 1, jnp.where(steps == 0, BLOCKS - 1, steps - 1))
        return copy(source, target, half, (sibling, head), 9 + steps + half)

    def arrived(steps, half):
        copy(steps, steps, half, (ctx, other), 0).wait_recv()

    def spread(steps):
        @pl.when(has_ahead(steps))
        def _():
            for plane in (0, 1):
                direct(steps, plane).start()

    def landed(steps):
        @pl.when(has_behind(steps))
        def _():
            for half in (0, 1):
                arrived(steps, half)

    def pass_on(steps):
        landed(steps)
        for half in (0, 1):
            across(steps, half).start()

    def pass_ends(lower):
        @pl.when(core == (1 if lower else 0))
        def _():
            for half in (0, 1):
                across(0, half).start()

    if remote:
        reached = sum(has_ahead(steps).astype(jnp.int32) for steps in REACH)
        pl.semaphore_wait(barrier, 2 + 2 * reached)
        to_partner().start()
        spread(2)
        spread(4)
        spread(6)
        spread(8)

    low = lane < 64
    front = (lane & 63) < 32

    def absorb(part, carry):
        load_up(part).wait()
        for p in range(per // 2):
            at = pl.multiple_of(part * (per * 64) + p * 128, 128)
            pairs = rope[:, pl.ds(at, 128)].astype(jnp.float32)
            swap = jnp.where(front, pltpu.roll(pairs, 96, 1), pltpu.roll(pairs, 32, 1))
            turn = pairs * cos_ref[...] + swap * sin_ref[...]
            for odd in range(2):
                h = part * per + 2 * p + odd
                own = pl.ds(pl.multiple_of(h * ROWS, ROWS), ROWS)
                query[own, LATENT:] = jnp.where(~low if odd else low, turn, 0.0).astype(jnp.bfloat16)
                query[own, :LATENT] = jnp.dot(
                    nope[:, pl.ds(pl.multiple_of(h * 128, 128), 128)], up[h], preferred_element_type=jnp.float32
                ).astype(jnp.bfloat16)
        return carry

    key = lax.broadcasted_iota(jnp.int32, (ROWS, 128), 1)
    for tile in range(BLOCKS):
        shifted = (ctx - (BLOCKS - 1) + tile) * ROWS + key
        bias[:, tile * 128 : (tile + 1) * 128] = jnp.where((shifted >= begin) & (shifted <= position), 0.0, -1e30)

    load_query().wait()
    load_rope().wait()
    for part in range(PARTS):
        lax.fori_loop(part, part + 1, absorb, 0)
    if remote:
        arrived(0, other)

    def scores(chunk):
        first = FAR - (chunk + 1) * CHUNK

        def band(step, carry):
            own = pl.ds(pl.multiple_of(step * TALL, TALL), TALL)
            s = lax.dot_general(
                query[own, :], kv[ROWS + CHUNK + first : ROWS + 2 * CHUNK + first, :], (((1,), (1,)), ((), ())),
                preferred_element_type=jnp.float32,
            )
            s = s.reshape(TALL // ROWS, ROWS, CHUNK) * (SCALE * LOG2E)
            s = (s + bias[:, CHUNK + first : 2 * CHUNK + first]).reshape(TALL, CHUNK)
            score[own, first : first + CHUNK] = s
            high = jnp.maximum(s[:, :128], s[:, 128:])
            peak[own, :] = jnp.maximum(peak[own, :], high) if chunk else high
            return carry

        lax.fori_loop(0, heads * ROWS // TALL, band, 0)

    def soften(step, weight):
        for piece in range(BAND // SLICE):
            at = piece * SLICE
            own = pl.ds(pl.multiple_of(step * BAND, BAND) + at, SLICE)
            top = jnp.broadcast_to(jnp.max(peak[own, :], axis=1, keepdims=True), (SLICE, 128))
            total = None
            for tile in range(FAR // 128):
                w = jnp.exp2(score[own, tile * 128 : (tile + 1) * 128] - top)
                total = w if total is None else total + w
                weight[at : at + SLICE, tile * 128 : (tile + 1) * 128] = w.astype(jnp.bfloat16)
            top_ref[own, :] = top
            sum_ref[own, :] = total

    def mix(step, weight):
        partial[pl.ds(pl.multiple_of(step * BAND, BAND), BAND), :] = jnp.dot(
            weight[...], kv[ROWS + CHUNK :, :LATENT], preferred_element_type=jnp.float32
        )

    def score_far(step, last):
        own = pl.ds(pl.multiple_of(step * BAND, BAND), BAND)
        s = lax.dot_general(
            query[own, :], kv[ROWS : ROWS + CHUNK, :], (((1,), (1,)), ((), ())), preferred_element_type=jnp.float32
        )
        s = s.reshape(GROUP, ROWS, CHUNK) * (SCALE * LOG2E) + bias[:, :CHUNK]
        last[...] = s.reshape(BAND, CHUNK)

    def soften_far(step, last, narrow, old, new):
        for piece in range(BAND // SLICE):
            at = piece * SLICE
            own = pl.ds(pl.multiple_of(step * BAND, BAND) + at, SLICE)
            s0, s1 = last[at : at + SLICE, :128], last[at : at + SLICE, 128:]
            before = top_ref[own, :]
            high = jnp.maximum(jnp.maximum(s0, s1), before)
            top = jnp.broadcast_to(jnp.max(high, axis=1, keepdims=True), (SLICE, 128))
            w0, w1 = jnp.exp2(s0 - top), jnp.exp2(s1 - top)
            fade = jnp.exp2(before - top)
            total = jnp.sum(sum_ref[own, :] * fade + w0 + w1, axis=1, keepdims=True)
            scale = jnp.broadcast_to(1.0 / total, (SLICE, 128))
            narrow[at : at + SLICE, :128] = w0.astype(jnp.bfloat16)
            narrow[at : at + SLICE, 128:] = w1.astype(jnp.bfloat16)
            new[at : at + SLICE, :] = scale
            old[at : at + SLICE, :] = scale * fade

    def finish(step, narrow, old, new):
        own = pl.ds(pl.multiple_of(step * BAND, BAND), BAND)
        mixed = jnp.dot(narrow[...], kv[ROWS : ROWS + CHUNK, :LATENT], preferred_element_type=jnp.float32)
        a, b = old[...], new[...]
        mixed = jnp.concatenate(
            [
                (partial[own, t : t + 128] * a + mixed[:, t : t + 128] * b).astype(jnp.bfloat16)
                for t in range(0, LATENT, 128)
            ],
            axis=1,
        )
        for h in range(GROUP):
            out[:, pl.ds(pl.multiple_of(step * BAND, BAND) + h * 128, 128)] = jnp.dot(
                mixed[h * ROWS : (h + 1) * ROWS], value[step * GROUP + h], preferred_element_type=jnp.float32
            ).astype(jnp.bfloat16)
        write(step).start()

    def write(step):
        own = pl.ds(pl.multiple_of(step * BAND, BAND), BAND)
        return pltpu.make_async_copy(out.at[:, own], out_hbm.at[:, own], out_sem.at[step])

    steps = heads // GROUP
    for chunk in range(KEYS // CHUNK):
        if remote:
            if chunk == 0:
                pass_ends(False)
            for steps_on in ((2, 4), (6,), (), ())[chunk]:
                pass_on(steps_on)
            if chunk == 2:
                landed(BLOCKS)
                pass_ends(True)
            for half in (0, 1):
                arrived(2 * chunk + 1, half)
        if chunk + 1 < KEYS // CHUNK:
            scores(chunk)
        if chunk + 2 == KEYS // CHUNK:
            soften(0, weight_a)

            def near(j, carry):
                soften(2 * j + 1, weight_b)
                mix(2 * j, weight_a)
                soften(2 * j + 2, weight_a)
                mix(2 * j + 1, weight_b)
                return carry

            lax.fori_loop(0, steps // 2 - 1, near, 0)
            soften(steps - 1, weight_b)
            mix(steps - 2, weight_a)
            mix(steps - 1, weight_b)

    load_value().wait()
    even, odd = (narrow_a, old_a, new_a), (narrow_b, old_b, new_b)
    score_far(0, last_a)
    score_far(1, last_b)
    soften_far(0, last_a, *even)

    def far(j, carry):
        score_far(2 * j + 2, last_a)
        soften_far(2 * j + 1, last_b, *odd)
        finish(2 * j, *even)
        score_far(2 * j + 3, last_b)
        soften_far(2 * j + 2, last_a, *even)
        finish(2 * j + 1, *odd)
        return carry

    lax.fori_loop(0, steps // 2 - 1, far, 0)
    soften_far(steps - 1, last_b, *odd)
    finish(steps - 2, *even)
    finish(steps - 1, *odd)
    for step in range(steps):
        write(step).wait()

    if remote:
        to_partner().wait_send()
        for half in (0, 1):
            for steps in REACH:

                @pl.when(has_ahead(steps))
                def _():
                    direct(steps, half).wait_send()

            for steps in (0, 2, 4, 6):
                across(steps, half).wait_send()


def shards(count, remote, latent_raw, kv_gain, query_nope, query_rope, key_up, value_up, doc_lengths):
    vmem, hbm = pl.BlockSpec(memory_space=pltpu.VMEM), pl.BlockSpec(memory_space=pl.ANY)
    heads = key_up.shape[0]
    bf16, f32 = jnp.bfloat16, jnp.float32
    return pl.pallas_call(
        functools.partial(latent_attention, count, heads, remote),
        out_shape=jax.ShapeDtypeStruct((ROWS, heads * 128), bf16),
        in_specs=[vmem, vmem, pl.BlockSpec(memory_space=pltpu.SMEM), hbm, hbm, hbm, hbm],
        out_specs=hbm,
        scratch_shapes=[
            pltpu.VMEM((ROWS + KEYS, WIDTH), bf16),
            pltpu.VMEM(query_nope.shape, bf16),
            pltpu.VMEM(query_rope.shape, bf16),
            pltpu.VMEM(key_up.shape, bf16),
            pltpu.VMEM(value_up.shape, bf16),
            pltpu.VMEM((heads * ROWS, WIDTH), bf16),
            pltpu.VMEM((heads * ROWS, FAR), f32),
            *[pltpu.VMEM((heads * ROWS, 128), f32)] * 3,
            pltpu.VMEM((heads * ROWS, LATENT), f32),
            *[pltpu.VMEM((BAND, CHUNK), f32)] * 2,
            *[pltpu.VMEM((BAND, FAR), bf16)] * 2,
            *[pltpu.VMEM((BAND, CHUNK), bf16)] * 2,
            *[pltpu.VMEM((BAND, 128), f32)] * 4,
            pltpu.VMEM((ROWS, KEYS), f32),
            pltpu.VMEM((ROWS, 128), f32),
            pltpu.VMEM((ROWS, 128), f32),
            pltpu.VMEM((ROWS, heads * 128), bf16),
            pltpu.SemaphoreType.DMA((23,)),
            pltpu.SemaphoreType.DMA((BLOCKS + 1, 2)),
            pltpu.SemaphoreType.DMA((3 + PARTS,)),
            pltpu.SemaphoreType.DMA((heads // GROUP,)),
        ],
        compiler_params=pltpu.CompilerParams(
            collective_id=0 if remote else None, has_side_effects=True, vmem_limit_bytes=60 << 20
        ),
        name="latent_attention",
    )(latent_raw, kv_gain[None, :], doc_lengths, query_nope, query_rope, key_up, value_up)


def solution(mesh):
    return jax.shard_map(
        functools.partial(shards, mesh.shape["ctx"], True),
        mesh=mesh,
        in_specs=(
            P(("ctx", "head"), None),
            P(),
            P("ctx", "head"),
            P("ctx", "head"),
            P("head", None, None),
            P("head", None, None),
            P(),
        ),
        out_specs=P("ctx", "head"),
        check_vma=False,
    )
```

```python
import functools
import math

import jax
import jax.numpy as jnp
from jax import lax
from jax.experimental import pallas as pl
from jax.experimental.pallas import tpu as pltpu
from jax.sharding import PartitionSpec as P

LATENT, WIDTH = 512, 640
ROWS, HALF, BLOCKS, DOCS = 128, 64, 8, 32
KEYS = BLOCKS * ROWS
SCALE = 192.0 ** -0.5
LOG2E = math.log2(math.e)
REACH = (2, 4, 6, 8)
CHUNK = 256
NEAR = 512
FAR = KEYS - NEAR
TALL = 2048
GROUP = 4
BAND = GROUP * ROWS
SLICE = 16
PARTS = 8
MESH = pl.DeviceIdType.MESH


def latent_attention(
    count, heads, remote, raw_ref, gain_ref, len_ref, nope_hbm, rope_hbm, up_hbm, value_hbm, out_hbm,
    kv, nope, rope, up, value, query, score, peak, top_ref, sum_ref, partial, last_a, last_b, weight_a, weight_b,
    narrow_a, narrow_b, old_a, old_b, new_a, new_b, bias, cos_ref, sin_ref, out,
    send_sem, recv_sem, load_sem, out_sem,
):
    ctx = lax.axis_index("ctx") if remote else 0
    head = lax.axis_index("head") if remote else 0
    core = lax.rem(ctx, 2)
    other = 1 - head
    sibling = ctx + 1 - 2 * core
    per = heads // PARTS

    def wanted(steps):
        return core == 1 if steps == BLOCKS else core >= 0

    def has_behind(steps):
        return jnp.logical_and(ctx >= steps, wanted(steps))

    def has_ahead(steps):
        return jnp.logical_and(ctx + steps < count, wanted(steps))

    if remote:
        barrier = pltpu.get_barrier_semaphore()

        def greet(where):
            pl.semaphore_signal(barrier, inc=1, device_id=where, device_id_type=MESH)

        @pl.when(ctx < BLOCKS)
        def _():
            kv[...] = jnp.zeros_like(kv)

        greet((ctx, other))
        greet((sibling, head))
        for steps in REACH:

            @pl.when(has_behind(steps))
            def _():
                for plane in (0, 1):
                    greet((ctx - steps, plane))

    def load_query():
        return pltpu.make_async_copy(nope_hbm, nope, load_sem.at[0])

    def load_rope():
        return pltpu.make_async_copy(rope_hbm, rope, load_sem.at[1])

    def load_up(part):
        own = pl.ds(part * per, per)
        return pltpu.make_async_copy(up_hbm.at[own], up.at[own], load_sem.at[2 + part])

    def load_value():
        return pltpu.make_async_copy(value_hbm, value, load_sem.at[2 + PARTS])

    load_query().start()
    load_rope().start()
    for part in range(PARTS):
        load_up(part).start()
    load_value().start()

    row = lax.broadcasted_iota(jnp.int32, (ROWS, 128), 0)
    lane = lax.broadcasted_iota(jnp.int32, (ROWS, 128), 1)
    position = ctx * ROWS + row
    begin = jnp.zeros((ROWS, 128), jnp.int32)
    start = jnp.int32(0)
    for doc in range(DOCS):
        begin = jnp.where(position >= start, start, begin)
        start = start + len_ref[doc]
    frequency = jnp.exp2((lane & 31).astype(jnp.float32) * (-math.log2(10000.0) / 32))
    angle = (position - begin).astype(jnp.float32) * frequency
    cos_ref[...] = jnp.cos(angle)
    sine = jnp.sin(angle)
    sin_ref[...] = jnp.where((lane & 63) < 32, -sine, sine)

    def half_at(steps, half):
        return pl.ds(pl.multiple_of((BLOCKS - steps) * ROWS + half * HALF, HALF), HALF)

    mine = half_at(0, head)
    latent = raw_ref[:, :LATENT].astype(jnp.float32)
    norm = lax.rsqrt(jnp.mean(latent * latent, axis=1, keepdims=True) + 1e-6)
    kv[mine, :LATENT] = (latent * norm * gain_ref[...]).astype(jnp.bfloat16)
    pair = raw_ref[:, LATENT:].astype(jnp.float32)
    swapped = jnp.concatenate([pair[:, 32:], pair[:, :32]], axis=1)
    table = pl.ds(pl.multiple_of(head * HALF, HALF), HALF)
    turned = pair * cos_ref[table, :64] + swapped * sin_ref[table, :64]
    kv[mine, LATENT:] = jnp.concatenate([turned, turned], axis=1).astype(jnp.bfloat16)

    def copy(source, target, half, where, send):
        return pltpu.make_async_remote_copy(
            src_ref=kv.at[half_at(source, half)],
            dst_ref=kv.at[half_at(target, half)],
            send_sem=send_sem.at[send],
            recv_sem=recv_sem.at[target, half],
            device_id=where,
            device_id_type=MESH,
        )

    def to_partner():
        return copy(0, 0, head, (ctx, other), 0)

    def direct(steps, plane):
        return copy(0, steps, head, (ctx + steps, plane), steps - 1 + plane)

    def across(steps, half):
        source = jnp.where((core == 1) & (steps == 0), BLOCKS, steps)
        target = jnp.where(core == 0, steps + 1, jnp.where(steps == 0, BLOCKS - 1, steps - 1))
        return copy(source, target, half, (sibling, head), 9 + steps + half)

    def arrived(steps, half):
        copy(steps, steps, half, (ctx, other), 0).wait_recv()

    def spread(steps):
        @pl.when(has_ahead(steps))
        def _():
            for plane in (0, 1):
                direct(steps, plane).start()

    def landed(steps):
        @pl.when(has_behind(steps))
        def _():
            for half in (0, 1):
                arrived(steps, half)

    def pass_on(steps):
        landed(steps)
        for half in (0, 1):
            across(steps, half).start()

    def pass_ends(lower):
        @pl.when(core == (1 if lower else 0))
        def _():
            for half in (0, 1):
                across(0, half).start()

    if remote:
        reached = sum(has_ahead(steps).astype(jnp.int32) for steps in REACH)
        pl.semaphore_wait(barrier, 2 + 2 * reached)
        to_partner().start()
        spread(2)
        spread(4)
        spread(6)
        spread(8)

    low = lane < 64
    front = (lane & 63) < 32

    def absorb(part, carry):
        load_up(part).wait()
        for p in range(per // 2):
            at = pl.multiple_of(part * (per * 64) + p * 128, 128)
            pairs = rope[:, pl.ds(at, 128)].astype(jnp.float32)
            swap = jnp.where(front, pltpu.roll(pairs, 96, 1), pltpu.roll(pairs, 32, 1))
            turn = pairs * cos_ref[...] + swap * sin_ref[...]
            for odd in range(2):
                h = part * per + 2 * p + odd
                own = pl.ds(pl.multiple_of(h * ROWS, ROWS), ROWS)
                query[own, LATENT:] = jnp.where(~low if odd else low, turn, 0.0).astype(jnp.bfloat16)
                query[own, :LATENT] = jnp.dot(
                    nope[:, pl.ds(pl.multiple_of(h * 128, 128), 128)], up[h], preferred_element_type=jnp.float32
                ).astype(jnp.bfloat16)
        return carry

    key = lax.broadcasted_iota(jnp.int32, (ROWS, 128), 1)
    for tile in range(BLOCKS):
        shifted = (ctx - (BLOCKS - 1) + tile) * ROWS + key
        bias[:, tile * 128 : (tile + 1) * 128] = jnp.where((shifted >= begin) & (shifted <= position), 0.0, -1e30)

    load_query().wait()
    load_rope().wait()
    lax.fori_loop(0, PARTS, absorb, 0)
    if remote:
        arrived(0, other)

    def scores(chunk):
        first = NEAR - (chunk + 1) * CHUNK

        def band(step, carry):
            own = pl.ds(pl.multiple_of(step * TALL, TALL), TALL)
            s = lax.dot_general(
                query[own, :], kv[ROWS + FAR + first : ROWS + FAR + first + CHUNK, :], (((1,), (1,)), ((), ())),
                preferred_element_type=jnp.float32,
            )
            s = s.reshape(TALL // ROWS, ROWS, CHUNK) * (SCALE * LOG2E)
            s = (s + bias[:, FAR + first : FAR + first + CHUNK]).reshape(TALL, CHUNK)
            score[own, first : first + CHUNK] = s
            high = jnp.maximum(s[:, :128], s[:, 128:])
            peak[own, :] = jnp.maximum(peak[own, :], high) if chunk else high
            return carry

        lax.fori_loop(0, heads * ROWS // TALL, band, 0)

    def soften(step, weight):
        for piece in range(BAND // SLICE):
            at = piece * SLICE
            own = pl.ds(pl.multiple_of(step * BAND, BAND) + at, SLICE)
            top = jnp.broadcast_to(jnp.max(peak[own, :], axis=1, keepdims=True), (SLICE, 128))
            total = None
            for tile in range(NEAR // 128):
                w = jnp.exp2(score[own, tile * 128 : (tile + 1) * 128] - top)
                total = w if total is None else total + w
                weight[at : at + SLICE, tile * 128 : (tile + 1) * 128] = w.astype(jnp.bfloat16)
            top_ref[own, :] = top
            sum_ref[own, :] = total

    def mix(step, weight):
        partial[pl.ds(pl.multiple_of(step * BAND, BAND), BAND), :] = jnp.dot(
            weight[...], kv[ROWS + FAR :, :LATENT], preferred_element_type=jnp.float32
        )

    def score_far(step, last):
        own = pl.ds(pl.multiple_of(step * BAND, BAND), BAND)
        s = lax.dot_general(
            query[own, :], kv[ROWS : ROWS + FAR, :], (((1,), (1,)), ((), ())), preferred_element_type=jnp.float32
        )
        s = s.reshape(GROUP, ROWS, FAR) * (SCALE * LOG2E) + bias[:, :FAR]
        last[...] = s.reshape(BAND, FAR)

    def soften_far(step, last, narrow, old, new):
        for piece in range(BAND // SLICE):
            at = piece * SLICE
            own = pl.ds(pl.multiple_of(step * BAND, BAND) + at, SLICE)
            before = top_ref[own, :]
            high = before
            for tile in range(0, FAR, 128):
                high = jnp.maximum(high, last[at : at + SLICE, tile : tile + 128])
            top = jnp.broadcast_to(jnp.max(high, axis=1, keepdims=True), (SLICE, 128))
            fade = jnp.exp2(before - top)
            total = sum_ref[own, :] * fade
            for tile in range(0, FAR, 128):
                w = jnp.exp2(last[at : at + SLICE, tile : tile + 128] - top)
                total = total + w
                narrow[at : at + SLICE, tile : tile + 128] = w.astype(jnp.bfloat16)
            total = jnp.sum(total, axis=1, keepdims=True)
            scale = jnp.broadcast_to(1.0 / total, (SLICE, 128))
            new[at : at + SLICE, :] = scale
            old[at : at + SLICE, :] = scale * fade

    def finish(step, narrow, old, new):
        own = pl.ds(pl.multiple_of(step * BAND, BAND), BAND)
        mixed = jnp.dot(narrow[...], kv[ROWS : ROWS + FAR, :LATENT], preferred_element_type=jnp.float32)
        a, b = old[...], new[...]
        mixed = jnp.concatenate(
            [
                (partial[own, t : t + 128] * a + mixed[:, t : t + 128] * b).astype(jnp.bfloat16)
                for t in range(0, LATENT, 128)
            ],
            axis=1,
        )
        for h in range(GROUP):
            out[:, pl.ds(pl.multiple_of(step * BAND, BAND) + h * 128, 128)] = jnp.dot(
                mixed[h * ROWS : (h + 1) * ROWS], value[step * GROUP + h], preferred_element_type=jnp.float32
            ).astype(jnp.bfloat16)
        write(step).start()

    def write(step):
        own = pl.ds(pl.multiple_of(step * BAND, BAND), BAND)
        return pltpu.make_async_copy(out.at[:, own], out_hbm.at[:, own], out_sem.at[step])

    steps = heads // GROUP
    for chunk in range(KEYS // CHUNK):
        if remote:
            if chunk == 0:
                pass_ends(False)
            for steps_on in ((2, 4), (6,), (), ())[chunk]:
                pass_on(steps_on)
            for half in (0, 1):
                arrived(2 * chunk + 1, half)
        if chunk < NEAR // CHUNK:
            scores(chunk)
        if remote and chunk == 1:
            landed(BLOCKS)
            pass_ends(True)
        if chunk + 1 == NEAR // CHUNK:
            soften(0, weight_a)

            def near(j, carry):
                soften(2 * j + 1, weight_b)
                mix(2 * j, weight_a)
                soften(2 * j + 2, weight_a)
                mix(2 * j + 1, weight_b)
                return carry

            lax.fori_loop(0, steps // 2 - 1, near, 0)
            soften(steps - 1, weight_b)
            mix(steps - 2, weight_a)
            mix(steps - 1, weight_b)

    load_value().wait()
    even, odd = (narrow_a, old_a, new_a), (narrow_b, old_b, new_b)
    score_far(0, last_a)
    score_far(1, last_b)
    soften_far(0, last_a, *even)

    def far(j, carry):
        score_far(2 * j + 2, last_a)
        soften_far(2 * j + 1, last_b, *odd)
        finish(2 * j, *even)
        score_far(2 * j + 3, last_b)
        soften_far(2 * j + 2, last_a, *even)
        finish(2 * j + 1, *odd)
        return carry

    lax.fori_loop(0, steps // 2 - 1, far, 0)
    soften_far(steps - 1, last_b, *odd)
    finish(steps - 2, *even)
    finish(steps - 1, *odd)
    for step in range(steps):
        write(step).wait()

    if remote:
        to_partner().wait_send()
        for half in (0, 1):
            for steps in REACH:

                @pl.when(has_ahead(steps))
                def _():
                    direct(steps, half).wait_send()

            for steps in (0, 2, 4, 6):
                across(steps, half).wait_send()


def shards(count, remote, latent_raw, kv_gain, query_nope, query_rope, key_up, value_up, doc_lengths):
    vmem, hbm = pl.BlockSpec(memory_space=pltpu.VMEM), pl.BlockSpec(memory_space=pl.ANY)
    heads = key_up.shape[0]
    bf16, f32 = jnp.bfloat16, jnp.float32
    return pl.pallas_call(
        functools.partial(latent_attention, count, heads, remote),
        out_shape=jax.ShapeDtypeStruct((ROWS, heads * 128), bf16),
        in_specs=[vmem, vmem, pl.BlockSpec(memory_space=pltpu.SMEM), hbm, hbm, hbm, hbm],
        out_specs=hbm,
        scratch_shapes=[
            pltpu.VMEM((ROWS + KEYS, WIDTH), bf16),
            pltpu.VMEM(query_nope.shape, bf16),
            pltpu.VMEM(query_rope.shape, bf16),
            pltpu.VMEM(key_up.shape, bf16),
            pltpu.VMEM(value_up.shape, bf16),
            pltpu.VMEM((heads * ROWS, WIDTH), bf16),
            pltpu.VMEM((heads * ROWS, NEAR), f32),
            *[pltpu.VMEM((heads * ROWS, 128), f32)] * 3,
            pltpu.VMEM((heads * ROWS, LATENT), f32),
            *[pltpu.VMEM((BAND, FAR), f32)] * 2,
            *[pltpu.VMEM((BAND, NEAR), bf16)] * 2,
            *[pltpu.VMEM((BAND, FAR), bf16)] * 2,
            *[pltpu.VMEM((BAND, 128), f32)] * 4,
            pltpu.VMEM((ROWS, KEYS), f32),
            pltpu.VMEM((ROWS, 128), f32),
            pltpu.VMEM((ROWS, 128), f32),
            pltpu.VMEM((ROWS, heads * 128), bf16),
            pltpu.SemaphoreType.DMA((23,)),
            pltpu.SemaphoreType.DMA((BLOCKS + 1, 2)),
            pltpu.SemaphoreType.DMA((3 + PARTS,)),
            pltpu.SemaphoreType.DMA((heads // GROUP,)),
        ],
        compiler_params=pltpu.CompilerParams(
            collective_id=0 if remote else None, has_side_effects=True, vmem_limit_bytes=60 << 20
        ),
        name="latent_attention",
    )(latent_raw, kv_gain[None, :], doc_lengths, query_nope, query_rope, key_up, value_up)


def solution(mesh):
    return jax.shard_map(
        functools.partial(shards, mesh.shape["ctx"], True),
        mesh=mesh,
        in_specs=(
            P(("ctx", "head"), None),
            P(),
            P("ctx", "head"),
            P("ctx", "head"),
            P("head", None, None),
            P("head", None, None),
            P(),
        ),
        out_specs=P("ctx", "head"),
        check_vma=False,
    )
```

```python
import functools
import math

import jax
import jax.numpy as jnp
from jax import lax
from jax.experimental import pallas as pl
from jax.experimental.pallas import tpu as pltpu
from jax.sharding import PartitionSpec as P

LATENT, WIDTH = 512, 640
ROWS, HALF, BLOCKS, DOCS = 128, 64, 8, 32
KEYS = BLOCKS * ROWS
SCALE = 192.0 ** -0.5
LOG2E = math.log2(math.e)
REACH = (2, 4, 6, 8)
CHUNK = 256
NEAR = 512
FAR = KEYS - NEAR
TALL = 2048
GROUP = 4
BAND = GROUP * ROWS
SLICE = 16
PARTS = 8
MESH = pl.DeviceIdType.MESH


def latent_attention(
    count, heads, remote, raw_ref, gain_ref, len_ref, nope_hbm, rope_hbm, up_hbm, value_hbm, out_hbm,
    kv, nope, rope, up, value, query, score, peak, top_ref, sum_ref, partial, last_a, last_b, weight_a, weight_b,
    narrow_a, narrow_b, old_a, old_b, new_a, new_b, bias, cos_ref, sin_ref, out,
    send_sem, recv_sem, load_sem, out_sem,
):
    ctx = lax.axis_index("ctx") if remote else 0
    head = lax.axis_index("head") if remote else 0
    core = lax.rem(ctx, 2)
    other = 1 - head
    sibling = ctx + 1 - 2 * core
    per = heads // PARTS

    def wanted(steps):
        return core == 1 if steps == BLOCKS else core >= 0

    def has_behind(steps):
        return jnp.logical_and(ctx >= steps, wanted(steps))

    def has_ahead(steps):
        return jnp.logical_and(ctx + steps < count, wanted(steps))

    if remote:
        barrier = pltpu.get_barrier_semaphore()

        def greet(where):
            pl.semaphore_signal(barrier, inc=1, device_id=where, device_id_type=MESH)

        @pl.when(ctx < BLOCKS)
        def _():
            kv[...] = jnp.zeros_like(kv)

        greet((ctx, other))
        greet((sibling, head))
        for steps in REACH:

            @pl.when(has_behind(steps))
            def _():
                for plane in (0, 1):
                    greet((ctx - steps, plane))

    def load_query():
        return pltpu.make_async_copy(nope_hbm, nope, load_sem.at[0])

    def load_rope():
        return pltpu.make_async_copy(rope_hbm, rope, load_sem.at[1])

    def load_up(part):
        own = pl.ds(part * per, per)
        return pltpu.make_async_copy(up_hbm.at[own], up.at[own], load_sem.at[2 + part])

    def load_value():
        return pltpu.make_async_copy(value_hbm, value, load_sem.at[2 + PARTS])

    load_query().start()
    load_rope().start()
    for part in range(PARTS):
        load_up(part).start()
    load_value().start()

    row = lax.broadcasted_iota(jnp.int32, (ROWS, 128), 0)
    lane = lax.broadcasted_iota(jnp.int32, (ROWS, 128), 1)
    position = ctx * ROWS + row
    begin = jnp.zeros((ROWS, 128), jnp.int32)
    start = jnp.int32(0)
    for doc in range(DOCS):
        begin = jnp.where(position >= start, start, begin)
        start = start + len_ref[doc]
    frequency = jnp.exp2((lane & 31).astype(jnp.float32) * (-math.log2(10000.0) / 32))
    angle = (position - begin).astype(jnp.float32) * frequency
    cos_ref[...] = jnp.cos(angle)
    sine = jnp.sin(angle)
    sin_ref[...] = jnp.where((lane & 63) < 32, -sine, sine)

    def half_at(steps, half):
        return pl.ds(pl.multiple_of((BLOCKS - steps) * ROWS + half * HALF, HALF), HALF)

    mine = half_at(0, head)
    latent = raw_ref[:, :LATENT].astype(jnp.float32)
    norm = lax.rsqrt(jnp.mean(latent * latent, axis=1, keepdims=True) + 1e-6)
    kv[mine, :LATENT] = (latent * norm * gain_ref[...]).astype(jnp.bfloat16)
    pair = raw_ref[:, LATENT:].astype(jnp.float32)
    swapped = jnp.concatenate([pair[:, 32:], pair[:, :32]], axis=1)
    table = pl.ds(pl.multiple_of(head * HALF, HALF), HALF)
    turned = pair * cos_ref[table, :64] + swapped * sin_ref[table, :64]
    kv[mine, LATENT:] = jnp.concatenate([turned, turned], axis=1).astype(jnp.bfloat16)

    def copy(source, target, half, where, send):
        return pltpu.make_async_remote_copy(
            src_ref=kv.at[half_at(source, half)],
            dst_ref=kv.at[half_at(target, half)],
            send_sem=send_sem.at[send],
            recv_sem=recv_sem.at[target, half],
            device_id=where,
            device_id_type=MESH,
        )

    def to_partner():
        return copy(0, 0, head, (ctx, other), 0)

    def direct(steps, plane):
        return copy(0, steps, head, (ctx + steps, plane), steps - 1 + plane)

    def across(steps, half):
        source = jnp.where((core == 1) & (steps == 0), BLOCKS, steps)
        target = jnp.where(core == 0, steps + 1, jnp.where(steps == 0, BLOCKS - 1, steps - 1))
        return copy(source, target, half, (sibling, head), 9 + steps + half)

    def arrived(steps, half):
        copy(steps, steps, half, (ctx, other), 0).wait_recv()

    def spread(steps):
        @pl.when(has_ahead(steps))
        def _():
            for plane in (head, other):
                direct(steps, plane).start()

    def landed(steps):
        @pl.when(has_behind(steps))
        def _():
            for half in (0, 1):
                arrived(steps, half)

    def pass_on(steps):
        landed(steps)
        for half in (0, 1):
            across(steps, half).start()

    def pass_ends(lower):
        @pl.when(core == (1 if lower else 0))
        def _():
            for half in (0, 1):
                across(0, half).start()

    if remote:
        reached = sum(has_ahead(steps).astype(jnp.int32) for steps in REACH)
        pl.semaphore_wait(barrier, 2 + 2 * reached)
        to_partner().start()
        spread(2)
        spread(4)
        spread(6)
        spread(8)

    low = lane < 64
    front = (lane & 63) < 32

    def absorb(part, carry):
        load_up(part).wait()
        for p in range(per // 2):
            at = pl.multiple_of(part * (per * 64) + p * 128, 128)
            pairs = rope[:, pl.ds(at, 128)].astype(jnp.float32)
            swap = jnp.where(front, pltpu.roll(pairs, 96, 1), pltpu.roll(pairs, 32, 1))
            turn = pairs * cos_ref[...] + swap * sin_ref[...]
            for odd in range(2):
                h = part * per + 2 * p + odd
                own = pl.ds(pl.multiple_of(h * ROWS, ROWS), ROWS)
                query[own, LATENT:] = jnp.where(~low if odd else low, turn, 0.0).astype(jnp.bfloat16)
                query[own, :LATENT] = jnp.dot(
                    nope[:, pl.ds(pl.multiple_of(h * 128, 128), 128)], up[h], preferred_element_type=jnp.float32
                ).astype(jnp.bfloat16)
        return carry

    key = lax.broadcasted_iota(jnp.int32, (ROWS, 128), 1)
    for tile in range(BLOCKS):
        shifted = (ctx - (BLOCKS - 1) + tile) * ROWS + key
        bias[:, tile * 128 : (tile + 1) * 128] = jnp.where((shifted >= begin) & (shifted <= position), 0.0, -1e30)

    load_query().wait()
    load_rope().wait()
    lax.fori_loop(0, PARTS, absorb, 0)
    if remote:
        arrived(0, other)

    def scores(chunk):
        first = NEAR - (chunk + 1) * CHUNK

        def band(step, carry):
            own = pl.ds(pl.multiple_of(step * TALL, TALL), TALL)
            s = lax.dot_general(
                query[own, :], kv[ROWS + FAR + first : ROWS + FAR + first + CHUNK, :], (((1,), (1,)), ((), ())),
                preferred_element_type=jnp.float32,
            )
            s = s.reshape(TALL // ROWS, ROWS, CHUNK) * (SCALE * LOG2E)
            s = (s + bias[:, FAR + first : FAR + first + CHUNK]).reshape(TALL, CHUNK)
            score[own, first : first + CHUNK] = s
            high = jnp.maximum(s[:, :128], s[:, 128:])
            peak[own, :] = jnp.maximum(peak[own, :], high) if chunk else high
            return carry

        lax.fori_loop(0, heads * ROWS // TALL, band, 0)

    def soften(step, weight):
        for piece in range(BAND // SLICE):
            at = piece * SLICE
            own = pl.ds(pl.multiple_of(step * BAND, BAND) + at, SLICE)
            top = jnp.broadcast_to(jnp.max(peak[own, :], axis=1, keepdims=True), (SLICE, 128))
            total = None
            for tile in range(NEAR // 128):
                w = jnp.exp2(score[own, tile * 128 : (tile + 1) * 128] - top)
                total = w if total is None else total + w
                weight[at : at + SLICE, tile * 128 : (tile + 1) * 128] = w.astype(jnp.bfloat16)
            top_ref[own, :] = top
            sum_ref[own, :] = total

    def mix(step, weight):
        partial[pl.ds(pl.multiple_of(step * BAND, BAND), BAND), :] = jnp.dot(
            weight[...], kv[ROWS + FAR :, :LATENT], preferred_element_type=jnp.float32
        )

    def score_far(step, last):
        own = pl.ds(pl.multiple_of(step * BAND, BAND), BAND)
        s = lax.dot_general(
            query[own, :], kv[ROWS : ROWS + FAR, :], (((1,), (1,)), ((), ())), preferred_element_type=jnp.float32
        )
        s = s.reshape(GROUP, ROWS, FAR) * (SCALE * LOG2E) + bias[:, :FAR]
        last[...] = s.reshape(BAND, FAR)

    def soften_far(step, last, narrow, old, new):
        for piece in range(BAND // SLICE):
            at = piece * SLICE
            own = pl.ds(pl.multiple_of(step * BAND, BAND) + at, SLICE)
            before = top_ref[own, :]
            high = before
            for tile in range(0, FAR, 128):
                high = jnp.maximum(high, last[at : at + SLICE, tile : tile + 128])
            top = jnp.broadcast_to(jnp.max(high, axis=1, keepdims=True), (SLICE, 128))
            fade = jnp.exp2(before - top)
            total = sum_ref[own, :] * fade
            for tile in range(0, FAR, 128):
                w = jnp.exp2(last[at : at + SLICE, tile : tile + 128] - top)
                total = total + w
                narrow[at : at + SLICE, tile : tile + 128] = w.astype(jnp.bfloat16)
            total = jnp.sum(total, axis=1, keepdims=True)
            scale = jnp.broadcast_to(1.0 / total, (SLICE, 128))
            new[at : at + SLICE, :] = scale
            old[at : at + SLICE, :] = scale * fade

    def finish(step, narrow, old, new):
        own = pl.ds(pl.multiple_of(step * BAND, BAND), BAND)
        mixed = jnp.dot(narrow[...], kv[ROWS : ROWS + FAR, :LATENT], preferred_element_type=jnp.float32)
        a, b = old[...], new[...]
        mixed = jnp.concatenate(
            [
                (partial[own, t : t + 128] * a + mixed[:, t : t + 128] * b).astype(jnp.bfloat16)
                for t in range(0, LATENT, 128)
            ],
            axis=1,
        )
        for h in range(GROUP):
            out[:, pl.ds(pl.multiple_of(step * BAND, BAND) + h * 128, 128)] = jnp.dot(
                mixed[h * ROWS : (h + 1) * ROWS], value[step * GROUP + h], preferred_element_type=jnp.float32
            ).astype(jnp.bfloat16)
        write(step).start()

    def write(step):
        own = pl.ds(pl.multiple_of(step * BAND, BAND), BAND)
        return pltpu.make_async_copy(out.at[:, own], out_hbm.at[:, own], out_sem.at[step])

    steps = heads // GROUP
    for chunk in range(KEYS // CHUNK):
        if remote:
            if chunk == 0:
                pass_ends(False)
            for steps_on in ((2,), (4, 6), (), ())[chunk]:
                pass_on(steps_on)
            for half in (0, 1):
                arrived(2 * chunk + 1, half)
        if chunk < NEAR // CHUNK:
            scores(chunk)
        if remote and chunk == 1:
            landed(BLOCKS)
            pass_ends(True)
        if chunk + 1 == NEAR // CHUNK:
            soften(0, weight_a)

            def near(j, carry):
                soften(2 * j + 1, weight_b)
                mix(2 * j, weight_a)
                soften(2 * j + 2, weight_a)
                mix(2 * j + 1, weight_b)
                return carry

            lax.fori_loop(0, steps // 2 - 1, near, 0)
            soften(steps - 1, weight_b)
            mix(steps - 2, weight_a)
            mix(steps - 1, weight_b)

    load_value().wait()
    even, odd = (narrow_a, old_a, new_a), (narrow_b, old_b, new_b)
    score_far(0, last_a)
    score_far(1, last_b)
    soften_far(0, last_a, *even)

    def far(j, carry):
        score_far(2 * j + 2, last_a)
        soften_far(2 * j + 1, last_b, *odd)
        finish(2 * j, *even)
        score_far(2 * j + 3, last_b)
        soften_far(2 * j + 2, last_a, *even)
        finish(2 * j + 1, *odd)
        return carry

    lax.fori_loop(0, steps // 2 - 1, far, 0)
    soften_far(steps - 1, last_b, *odd)
    finish(steps - 2, *even)
    finish(steps - 1, *odd)
    for step in range(steps):
        write(step).wait()

    if remote:
        to_partner().wait_send()
        for half in (0, 1):
            for steps in REACH:

                @pl.when(has_ahead(steps))
                def _():
                    direct(steps, half).wait_send()

            for steps in (0, 2, 4, 6):
                across(steps, half).wait_send()


def shards(count, remote, latent_raw, kv_gain, query_nope, query_rope, key_up, value_up, doc_lengths):
    vmem, hbm = pl.BlockSpec(memory_space=pltpu.VMEM), pl.BlockSpec(memory_space=pl.ANY)
    heads = key_up.shape[0]
    bf16, f32 = jnp.bfloat16, jnp.float32
    return pl.pallas_call(
        functools.partial(latent_attention, count, heads, remote),
        out_shape=jax.ShapeDtypeStruct((ROWS, heads * 128), bf16),
        in_specs=[vmem, vmem, pl.BlockSpec(memory_space=pltpu.SMEM), hbm, hbm, hbm, hbm],
        out_specs=hbm,
        scratch_shapes=[
            pltpu.VMEM((ROWS + KEYS, WIDTH), bf16),
            pltpu.VMEM(query_nope.shape, bf16),
            pltpu.VMEM(query_rope.shape, bf16),
            pltpu.VMEM(key_up.shape, bf16),
            pltpu.VMEM(value_up.shape, bf16),
            pltpu.VMEM((heads * ROWS, WIDTH), bf16),
            pltpu.VMEM((heads * ROWS, NEAR), f32),
            *[pltpu.VMEM((heads * ROWS, 128), f32)] * 3,
            pltpu.VMEM((heads * ROWS, LATENT), f32),
            *[pltpu.VMEM((BAND, FAR), f32)] * 2,
            *[pltpu.VMEM((BAND, NEAR), bf16)] * 2,
            *[pltpu.VMEM((BAND, FAR), bf16)] * 2,
            *[pltpu.VMEM((BAND, 128), f32)] * 4,
            pltpu.VMEM((ROWS, KEYS), f32),
            pltpu.VMEM((ROWS, 128), f32),
            pltpu.VMEM((ROWS, 128), f32),
            pltpu.VMEM((ROWS, heads * 128), bf16),
            pltpu.SemaphoreType.DMA((23,)),
            pltpu.SemaphoreType.DMA((BLOCKS + 1, 2)),
            pltpu.SemaphoreType.DMA((3 + PARTS,)),
            pltpu.SemaphoreType.DMA((heads // GROUP,)),
        ],
        compiler_params=pltpu.CompilerParams(
            collective_id=0 if remote else None, has_side_effects=True, vmem_limit_bytes=60 << 20
        ),
        name="latent_attention",
    )(latent_raw, kv_gain[None, :], doc_lengths, query_nope, query_rope, key_up, value_up)


def solution(mesh):
    return jax.shard_map(
        functools.partial(shards, mesh.shape["ctx"], True),
        mesh=mesh,
        in_specs=(
            P(("ctx", "head"), None),
            P(),
            P("ctx", "head"),
            P("ctx", "head"),
            P("head", None, None),
            P("head", None, None),
            P(),
        ),
        out_specs=P("ctx", "head"),
        check_vma=False,
    )
```

```python
import functools
import math

import jax
import jax.numpy as jnp
from jax import lax
from jax.experimental import pallas as pl
from jax.experimental.pallas import tpu as pltpu
from jax.sharding import PartitionSpec as P

LATENT, WIDTH = 512, 640
ROWS, HALF, BLOCKS, DOCS = 128, 64, 8, 32
KEYS = BLOCKS * ROWS
SCALE = 192.0 ** -0.5
LOG2E = math.log2(math.e)
REACH = (2, 4, 6, 8)
CHUNK = 256
NEAR = 512
FAR = KEYS - NEAR
TALL = 2048
GROUP = 4
BAND = GROUP * ROWS
SLICE = 16
PARTS = 8
MESH = pl.DeviceIdType.MESH


def latent_attention(
    count, heads, remote, raw_ref, gain_ref, len_ref, nope_hbm, rope_hbm, up_hbm, value_hbm, out_hbm,
    kv, nope, rope, up, value, query, score, peak, top_ref, sum_ref, partial, last_a, last_b, weight_a, weight_b,
    narrow_a, narrow_b, old_a, old_b, new_a, new_b, bias, cos_ref, sin_ref, out,
    send_sem, recv_sem, load_sem, out_sem,
):
    ctx = lax.axis_index("ctx") if remote else 0
    head = lax.axis_index("head") if remote else 0
    core = lax.rem(ctx, 2)
    other = 1 - head
    sibling = ctx + 1 - 2 * core
    per = heads // PARTS

    def wanted(steps):
        return core == 1 if steps == BLOCKS else core >= 0

    def has_behind(steps):
        return jnp.logical_and(ctx >= steps, wanted(steps))

    def has_ahead(steps):
        return jnp.logical_and(ctx + steps < count, wanted(steps))

    if remote:
        barrier = pltpu.get_barrier_semaphore()

        def greet(where):
            pl.semaphore_signal(barrier, inc=1, device_id=where, device_id_type=MESH)

        @pl.when(ctx < BLOCKS)
        def _():
            kv[...] = jnp.zeros_like(kv)

        greet((ctx, other))
        greet((sibling, head))
        for steps in REACH:

            @pl.when(has_behind(steps))
            def _():
                for plane in (0, 1):
                    greet((ctx - steps, plane))

    def load_query():
        return pltpu.make_async_copy(nope_hbm, nope, load_sem.at[0])

    def load_rope():
        return pltpu.make_async_copy(rope_hbm, rope, load_sem.at[1])

    def load_up(part):
        own = pl.ds(part * per, per)
        return pltpu.make_async_copy(up_hbm.at[own], up.at[own], load_sem.at[2 + part])

    def load_value():
        return pltpu.make_async_copy(value_hbm, value, load_sem.at[2 + PARTS])

    load_query().start()
    load_rope().start()
    for part in range(PARTS):
        load_up(part).start()
    load_value().start()

    row = lax.broadcasted_iota(jnp.int32, (ROWS, 128), 0)
    lane = lax.broadcasted_iota(jnp.int32, (ROWS, 128), 1)
    position = ctx * ROWS + row
    begin = jnp.zeros((ROWS, 128), jnp.int32)
    start = jnp.int32(0)
    for doc in range(DOCS):
        begin = jnp.where(position >= start, start, begin)
        start = start + len_ref[doc]
    frequency = jnp.exp2((lane & 31).astype(jnp.float32) * (-math.log2(10000.0) / 32))
    angle = (position - begin).astype(jnp.float32) * frequency
    cos_ref[...] = jnp.cos(angle)
    sine = jnp.sin(angle)
    sin_ref[...] = jnp.where((lane & 63) < 32, -sine, sine)

    def half_at(steps, half):
        return pl.ds(pl.multiple_of((BLOCKS - steps) * ROWS + half * HALF, HALF), HALF)

    mine = half_at(0, head)
    latent = raw_ref[:, :LATENT].astype(jnp.float32)
    norm = lax.rsqrt(jnp.mean(latent * latent, axis=1, keepdims=True) + 1e-6)
    kv[mine, :LATENT] = (latent * norm * gain_ref[...]).astype(jnp.bfloat16)
    pair = raw_ref[:, LATENT:].astype(jnp.float32)
    swapped = jnp.concatenate([pair[:, 32:], pair[:, :32]], axis=1)
    table = pl.ds(pl.multiple_of(head * HALF, HALF), HALF)
    turned = pair * cos_ref[table, :64] + swapped * sin_ref[table, :64]
    kv[mine, LATENT:] = jnp.concatenate([turned, turned], axis=1).astype(jnp.bfloat16)

    def copy(source, target, half, where, send):
        return pltpu.make_async_remote_copy(
            src_ref=kv.at[half_at(source, half)],
            dst_ref=kv.at[half_at(target, half)],
            send_sem=send_sem.at[send],
            recv_sem=recv_sem.at[target, half],
            device_id=where,
            device_id_type=MESH,
        )

    def to_partner():
        return copy(0, 0, head, (ctx, other), 0)

    def direct(steps, plane):
        return copy(0, steps, head, (ctx + steps, plane), steps - 1 + plane)

    def across(steps, half):
        source = jnp.where((core == 1) & (steps == 0), BLOCKS, steps)
        target = jnp.where(core == 0, steps + 1, jnp.where(steps == 0, BLOCKS - 1, steps - 1))
        return copy(source, target, half, (sibling, head), 9 + steps + half)

    def arrived(steps, half):
        copy(steps, steps, half, (ctx, other), 0).wait_recv()

    def spread(steps):
        @pl.when(has_ahead(steps))
        def _():
            for plane in (head, other):
                direct(steps, plane).start()

    def landed(steps):
        @pl.when(has_behind(steps))
        def _():
            for half in (0, 1):
                arrived(steps, half)

    def pass_on(steps):
        landed(steps)
        for half in (0, 1):
            across(steps, half).start()

    def pass_ends(lower):
        @pl.when(core == (1 if lower else 0))
        def _():
            for half in (0, 1):
                across(0, half).start()

    if remote:
        reached = sum(has_ahead(steps).astype(jnp.int32) for steps in REACH)
        pl.semaphore_wait(barrier, 2 + 2 * reached)
        spread(2)
        to_partner().start()
        spread(4)
        spread(6)
        spread(8)

    low = lane < 64
    front = (lane & 63) < 32

    def absorb(part, carry):
        load_up(part).wait()
        for p in range(per // 2):
            at = pl.multiple_of(part * (per * 64) + p * 128, 128)
            pairs = rope[:, pl.ds(at, 128)].astype(jnp.float32)
            swap = jnp.where(front, pltpu.roll(pairs, 96, 1), pltpu.roll(pairs, 32, 1))
            turn = pairs * cos_ref[...] + swap * sin_ref[...]
            for odd in range(2):
                h = part * per + 2 * p + odd
                own = pl.ds(pl.multiple_of(h * ROWS, ROWS), ROWS)
                query[own, LATENT:] = jnp.where(~low if odd else low, turn, 0.0).astype(jnp.bfloat16)
                query[own, :LATENT] = jnp.dot(
                    nope[:, pl.ds(pl.multiple_of(h * 128, 128), 128)], up[h], preferred_element_type=jnp.float32
                ).astype(jnp.bfloat16)
        return carry

    key = lax.broadcasted_iota(jnp.int32, (ROWS, 128), 1)
    for tile in range(BLOCKS):
        shifted = (ctx - (BLOCKS - 1) + tile) * ROWS + key
        bias[:, tile * 128 : (tile + 1) * 128] = jnp.where((shifted >= begin) & (shifted <= position), 0.0, -1e30)

    load_query().wait()
    load_rope().wait()
    lax.fori_loop(0, PARTS, absorb, 0)
    if remote:
        arrived(0, other)

    def scores(chunk):
        first = NEAR - (chunk + 1) * CHUNK

        def band(step, carry):
            own = pl.ds(pl.multiple_of(step * TALL, TALL), TALL)
            s = lax.dot_general(
                query[own, :], kv[ROWS + FAR + first : ROWS + FAR + first + CHUNK, :], (((1,), (1,)), ((), ())),
                preferred_element_type=jnp.float32,
            )
            s = s.reshape(TALL // ROWS, ROWS, CHUNK) * (SCALE * LOG2E)
            s = (s + bias[:, FAR + first : FAR + first + CHUNK]).reshape(TALL, CHUNK)
            score[own, first : first + CHUNK] = s
            high = jnp.maximum(s[:, :128], s[:, 128:])
            peak[own, :] = jnp.maximum(peak[own, :], high) if chunk else high
            return carry

        lax.fori_loop(0, heads * ROWS // TALL, band, 0)

    def soften(step, weight):
        for piece in range(BAND // SLICE):
            at = piece * SLICE
            own = pl.ds(pl.multiple_of(step * BAND, BAND) + at, SLICE)
            top = jnp.broadcast_to(jnp.max(peak[own, :], axis=1, keepdims=True), (SLICE, 128))
            total = None
            for tile in range(NEAR // 128):
                w = jnp.exp2(score[own, tile * 128 : (tile + 1) * 128] - top)
                total = w if total is None else total + w
                weight[at : at + SLICE, tile * 128 : (tile + 1) * 128] = w.astype(jnp.bfloat16)
            top_ref[own, :] = top
            sum_ref[own, :] = total

    def mix(step, weight):
        partial[pl.ds(pl.multiple_of(step * BAND, BAND), BAND), :] = jnp.dot(
            weight[...], kv[ROWS + FAR :, :LATENT], preferred_element_type=jnp.float32
        )

    def score_far(step, last):
        own = pl.ds(pl.multiple_of(step * BAND, BAND), BAND)
        s = lax.dot_general(
            query[own, :], kv[ROWS : ROWS + FAR, :], (((1,), (1,)), ((), ())), preferred_element_type=jnp.float32
        )
        s = s.reshape(GROUP, ROWS, FAR) * (SCALE * LOG2E) + bias[:, :FAR]
        last[...] = s.reshape(BAND, FAR)

    def soften_far(step, last, narrow, old, new):
        for piece in range(BAND // SLICE):
            at = piece * SLICE
            own = pl.ds(pl.multiple_of(step * BAND, BAND) + at, SLICE)
            before = top_ref[own, :]
            high = before
            for tile in range(0, FAR, 128):
                high = jnp.maximum(high, last[at : at + SLICE, tile : tile + 128])
            top = jnp.broadcast_to(jnp.max(high, axis=1, keepdims=True), (SLICE, 128))
            fade = jnp.exp2(before - top)
            total = sum_ref[own, :] * fade
            for tile in range(0, FAR, 128):
                w = jnp.exp2(last[at : at + SLICE, tile : tile + 128] - top)
                total = total + w
                narrow[at : at + SLICE, tile : tile + 128] = w.astype(jnp.bfloat16)
            total = jnp.sum(total, axis=1, keepdims=True)
            scale = jnp.broadcast_to(1.0 / total, (SLICE, 128))
            new[at : at + SLICE, :] = scale
            old[at : at + SLICE, :] = scale * fade

    def finish(step, narrow, old, new):
        own = pl.ds(pl.multiple_of(step * BAND, BAND), BAND)
        mixed = jnp.dot(narrow[...], kv[ROWS : ROWS + FAR, :LATENT], preferred_element_type=jnp.float32)
        a, b = old[...], new[...]
        mixed = jnp.concatenate(
            [
                (partial[own, t : t + 128] * a + mixed[:, t : t + 128] * b).astype(jnp.bfloat16)
                for t in range(0, LATENT, 128)
            ],
            axis=1,
        )
        for h in range(GROUP):
            out[:, pl.ds(pl.multiple_of(step * BAND, BAND) + h * 128, 128)] = jnp.dot(
                mixed[h * ROWS : (h + 1) * ROWS], value[step * GROUP + h], preferred_element_type=jnp.float32
            ).astype(jnp.bfloat16)
        write(step).start()

    def write(step):
        own = pl.ds(pl.multiple_of(step * BAND, BAND), BAND)
        return pltpu.make_async_copy(out.at[:, own], out_hbm.at[:, own], out_sem.at[step])

    steps = heads // GROUP
    for chunk in range(KEYS // CHUNK):
        if remote:
            if chunk == 0:
                pass_ends(False)
            for steps_on in ((2,), (4, 6), (), ())[chunk]:
                pass_on(steps_on)
            for half in (0, 1):
                arrived(2 * chunk + 1, half)
        if chunk < NEAR // CHUNK:
            scores(chunk)
        if remote and chunk == 1:
            landed(BLOCKS)
            pass_ends(True)
        if chunk + 1 == NEAR // CHUNK:
            soften(0, weight_a)

            def near(j, carry):
                soften(2 * j + 1, weight_b)
                mix(2 * j, weight_a)
                soften(2 * j + 2, weight_a)
                mix(2 * j + 1, weight_b)
                return carry

            lax.fori_loop(0, steps // 2 - 1, near, 0)
            soften(steps - 1, weight_b)
            mix(steps - 2, weight_a)
            mix(steps - 1, weight_b)

    load_value().wait()
    even, odd = (narrow_a, old_a, new_a), (narrow_b, old_b, new_b)
    score_far(0, last_a)
    score_far(1, last_b)
    soften_far(0, last_a, *even)

    def far(j, carry):
        score_far(2 * j + 2, last_a)
        soften_far(2 * j + 1, last_b, *odd)
        finish(2 * j, *even)
        score_far(2 * j + 3, last_b)
        soften_far(2 * j + 2, last_a, *even)
        finish(2 * j + 1, *odd)
        return carry

    lax.fori_loop(0, steps // 2 - 1, far, 0)
    soften_far(steps - 1, last_b, *odd)
    finish(steps - 2, *even)
    finish(steps - 1, *odd)
    for step in range(steps):
        write(step).wait()

    if remote:
        to_partner().wait_send()
        for half in (0, 1):
            for steps in REACH:

                @pl.when(has_ahead(steps))
                def _():
                    direct(steps, half).wait_send()

            for steps in (0, 2, 4, 6):
                across(steps, half).wait_send()


def shards(count, remote, latent_raw, kv_gain, query_nope, query_rope, key_up, value_up, doc_lengths):
    vmem, hbm = pl.BlockSpec(memory_space=pltpu.VMEM), pl.BlockSpec(memory_space=pl.ANY)
    heads = key_up.shape[0]
    bf16, f32 = jnp.bfloat16, jnp.float32
    return pl.pallas_call(
        functools.partial(latent_attention, count, heads, remote),
        out_shape=jax.ShapeDtypeStruct((ROWS, heads * 128), bf16),
        in_specs=[vmem, vmem, pl.BlockSpec(memory_space=pltpu.SMEM), hbm, hbm, hbm, hbm],
        out_specs=hbm,
        scratch_shapes=[
            pltpu.VMEM((ROWS + KEYS, WIDTH), bf16),
            pltpu.VMEM(query_nope.shape, bf16),
            pltpu.VMEM(query_rope.shape, bf16),
            pltpu.VMEM(key_up.shape, bf16),
            pltpu.VMEM(value_up.shape, bf16),
            pltpu.VMEM((heads * ROWS, WIDTH), bf16),
            pltpu.VMEM((heads * ROWS, NEAR), f32),
            *[pltpu.VMEM((heads * ROWS, 128), f32)] * 3,
            pltpu.VMEM((heads * ROWS, LATENT), f32),
            *[pltpu.VMEM((BAND, FAR), f32)] * 2,
            *[pltpu.VMEM((BAND, NEAR), bf16)] * 2,
            *[pltpu.VMEM((BAND, FAR), bf16)] * 2,
            *[pltpu.VMEM((BAND, 128), f32)] * 4,
            pltpu.VMEM((ROWS, KEYS), f32),
            pltpu.VMEM((ROWS, 128), f32),
            pltpu.VMEM((ROWS, 128), f32),
            pltpu.VMEM((ROWS, heads * 128), bf16),
            pltpu.SemaphoreType.DMA((23,)),
            pltpu.SemaphoreType.DMA((BLOCKS + 1, 2)),
            pltpu.SemaphoreType.DMA((3 + PARTS,)),
            pltpu.SemaphoreType.DMA((heads // GROUP,)),
        ],
        compiler_params=pltpu.CompilerParams(
            collective_id=0 if remote else None, has_side_effects=True, vmem_limit_bytes=60 << 20
        ),
        name="latent_attention",
    )(latent_raw, kv_gain[None, :], doc_lengths, query_nope, query_rope, key_up, value_up)


def solution(mesh):
    return jax.shard_map(
        functools.partial(shards, mesh.shape["ctx"], True),
        mesh=mesh,
        in_specs=(
            P(("ctx", "head"), None),
            P(),
            P("ctx", "head"),
            P("ctx", "head"),
            P("head", None, None),
            P("head", None, None),
            P(),
        ),
        out_specs=P("ctx", "head"),
        check_vma=False,
    )
```
